32 devices in a mesh: row: 4 (over y, core), col: 2 (over x), depth: 4 (over z).
Axes of the slice: x: 2, y: 2, z: 4, core: 2. Of those that a mesh axis runs over, the one named last changes fastest.
Arguments:
- density: float32 [512, 5, 128, 128], P(('row', 'depth'), None, 'col'), may hold values from -0.6 to 0.6
- pattern: int32 [512, 5], P(('row', 'depth')), may hold values 0 or 1
Outputs:
- purified: float32 [512, 5, 128, 128], P(('row', 'depth'), None, 'col')
The draws below stay inside these ranges and needn't reach their ends.
All inputs are finite; a program needn't handle non-finite values. No bound on the sum of `pattern` on one device may be relied on, other than what follows from the above.
Results may differ from the reference program's by a relative error of at most 0.0001.
Values sent between devices are 32-bit elements; how exact they have to be, the bound alone decides.
A program may use at most 64 MiB of HBM per device.

```python
import jax
import jax.numpy as jnp
from jax import lax

BLOCK = 128
HALF = 2
BLOCKS = 512
WIDE = 5


def with_ends(drawn, key, low, high):
    place = [jax.random.randint(jax.random.fold_in(key, axis), (), 0, length) for axis, length in enumerate(drawn.shape)]
    main_axis = drawn.shape.index(max(drawn.shape))
    neighbour = place[:main_axis] + [(place[main_axis] + 1) % drawn.shape[main_axis]] + place[main_axis + 1:]
    return drawn.at[tuple(place)].set(low).at[tuple(neighbour)].set(high)


def shard_levels(own_key, extent, pieces, smallest, top_value):
    def one(dim, shards_of):
        heights = jax.random.uniform(jax.random.fold_in(jax.random.fold_in(own_key, 6), dim), (shards_of,), jnp.float32, smallest / len(pieces), top_value / len(pieces))
        return jnp.repeat(jnp.exp(heights), extent[dim] // shards_of).reshape((-1,) + (1,) * (len(extent) - dim - 1))

    gain = one(*pieces[0])
    for cut in pieces[1:]:
        gain = gain * one(*cut)
    return gain


def bell_draw(key, dims, deviation, reach, shards=(), dtype=jnp.bfloat16):
    entries = jax.random.normal(key, dims, jnp.float32) * deviation
    if len(shards) > 0:
        entries = shard_levels(key, dims, shards, -0.22, 0.18) * entries
    return jnp.clip(entries, min=-reach, max=reach).astype(dtype)


def setup_inputs(seed: int = 0) -> dict:
    key_list = jax.random.split(jax.random.key(seed), 3)
    density = bell_draw(key_list[0], (BLOCKS, WIDE, BLOCK, BLOCK), 0.1, 0.6, ((0, 16), (2, 2)), jnp.float32)
    pattern = with_ends((jax.random.randint(key_list[1], (BLOCKS, WIDE), 0, 4) < 3).astype(jnp.int32), jax.random.fold_in(key_list[1], 1), 0, 1)
    return dict(density=density, pattern=pattern)


def banded_product(left_tiles, other_tiles, pattern):
    summed = jnp.zeros(left_tiles.shape, jnp.float32)
    for source in range(WIDE):
        first_slot = max(0, source - HALF)
        last_slot = min(WIDE, source + HALF + 1)
        shifted = jnp.roll(other_tiles, -(source - HALF), axis=0)
        partner = shifted[:, first_slot - source + HALF:last_slot - source + HALF]
        contrib = jnp.einsum("iab,itbc->itac", left_tiles[:, source], partner, precision=lax.Precision.HIGHEST)
        summed = summed.at[:, first_slot:last_slot].add(contrib)
    return summed * pattern[:, :, None, None].astype(jnp.float32)


def reference(density, pattern):
    masked = density * pattern[:, :, None, None].astype(jnp.float32)
    square = banded_product(masked, masked, pattern)
    cube = banded_product(square, masked, pattern)
    return 3.0 * square - 2.0 * cube
```

```python
import functools

import jax
import jax.numpy as jnp
from jax import lax
from jax.experimental import pallas as pl
from jax.experimental.pallas import tpu as pltpu
from jax.sharding import PartitionSpec as P

MESH = pl.DeviceIdType.MESH
WIDE = 5
SLOTS = 6
RING = ("row", "depth")


def split(value):
    high = value.astype(jnp.bfloat16)
    low = (value - high.astype(jnp.float32)).astype(jnp.bfloat16)
    return high, low


def dot(a, b):
    return jnp.dot(a, b, preferred_element_type=jnp.float32)


def kernel(cols, ring, dens, mask, out, raw, masks, high, low, done,
           local_sem, mask_sem, send_sem, recv_sem, edge_send, edge_recv,
           relay_send, relay_recv, mask_send, mask_recv, out_sem):
    pairs = dens.shape[0]
    h = dens.shape[3]
    block = dens.shape[4]
    two = 2 * block
    last = pairs + 1
    me = lax.axis_index("col")
    depth = lax.axis_size("depth")
    place = lax.axis_index("row") * depth + lax.axis_index("depth")

    def on_ring(shift):
        at = lax.rem(place + shift + ring, ring)
        return {"row": at // depth, "depth": lax.rem(at, depth)}

    prev, following = on_ring(-1), on_ring(1)

    def peer(step):
        return {"col": lax.rem(me + step, cols)}

    def source(step):
        return lax.rem(me + cols - step, cols)

    def own(j):
        return pltpu.make_async_copy(dens.at[j - 1], raw.at[me, j], local_sem.at[j - 1])

    def across(step, j):
        return pltpu.make_async_remote_copy(
            dens.at[j - 1], raw.at[me, j], send_sem.at[step - 1, j - 1],
            recv_sem.at[step - 1, j - 1], device_id=peer(step), device_id_type=MESH)

    ends = ((pairs, 0, following), (1, last, prev))

    def edge(side):
        j, slot, device = ends[side]
        return pltpu.make_async_remote_copy(
            dens.at[j - 1], raw.at[me, slot], edge_send.at[side], edge_recv.at[side],
            device_id=device, device_id_type=MESH)

    def relay(side, step):
        j, slot, device = ends[side]
        return pltpu.make_async_remote_copy(
            raw.at[source(step), j], raw.at[source(step), slot], relay_send.at[side, step - 1],
            relay_recv.at[side, step - 1], device_id=device, device_id_type=MESH)

    def mask_edge(side):
        j, slot, device = ends[side]
        return pltpu.make_async_remote_copy(
            mask.at[j - 1], masks.at[slot], mask_send.at[side], mask_recv.at[side],
            device_id=device, device_id_type=MESH)

    def result(j):
        return pltpu.make_async_copy(done.at[j - 1], out.at[j - 1], out_sem.at[j - 1])

    steps = range(1, cols)

    barrier = pltpu.get_barrier_semaphore()
    for device in [peer(s) for s in steps] + [prev, following]:
        pl.semaphore_signal(barrier, inc=1, device_id=device, device_id_type=MESH)
    own_mask = pltpu.make_async_copy(mask, masks.at[pl.ds(1, pairs)], mask_sem)
    own_mask.start()
    pl.semaphore_wait(barrier, cols - 1 + 2)

    for j in (1, pairs):
        for s in steps:
            across(s, j).start()
    for side in (0, 1):
        mask_edge(side).start()
        edge(side).start()

    @pl.loop(2, pairs)
    def _(j):
        for s in steps:
            across(s, j).start()

    @pl.loop(1, pairs + 1)
    def _(j):
        own(j).start()

    def convert(j):
        for p in range(2):
            for s in range(WIDE):
                slot = p + s
                factor = masks[j, p:p + 1, slot * block:(slot + 1) * block]
                for c in range(cols):
                    a, b = split(raw[c, j, p, s] * factor)
                    rows = slice(p * block + c * h, p * block + (c + 1) * h)
                    lanes = slice(slot * block, (slot + 1) * block)
                    high[j, rows, lanes] = a
                    low[j, rows, lanes] = b
            empty = slice(0, block) if p else slice(WIDE * block, SLOTS * block)
            nothing = jnp.zeros((block, block), jnp.bfloat16)
            high[j, p * block:(p + 1) * block, empty] = nothing
            low[j, p * block:(p + 1) * block, empty] = nothing

    def product(j, a, b):
        both = jnp.concatenate([a, b], axis=0)
        m = a.shape[0]
        parts = []
        for n in range(3):
            total = None
            for k in range(3):
                at = n - k + 1
                if at < 0 or at > 2:
                    continue
                lanes = slice(at * two, (at + 1) * two)
                ks = slice(k * two, (k + 1) * two)
                stacked = dot(both[:, ks], high[j + k - 1, :, lanes])
                term = stacked[:m] + stacked[m:] + dot(a[:, ks], low[j + k - 1, :, lanes])
                total = term if total is None else total + term
            parts.append(total)
        return jnp.concatenate(parts, axis=1)

    def compute(j):
        def own_rows(ref):
            return jnp.concatenate(
                [ref[j, pl.ds(pl.multiple_of(p * block + me * h, h), h), :] for p in range(2)], axis=0)

        factor = jnp.concatenate(
            [jnp.broadcast_to(masks[j, p:p + 1, :], (h, SLOTS * block)) for p in range(2)], axis=0)
        square = product(j, own_rows(high), own_rows(low)) * factor
        cube = product(j, *split(square)) * factor
        value = 3.0 * square - 2.0 * cube
        for p in range(2):
            for s in range(WIDE):
                done[j - 1, p, s] = value[p * h:(p + 1) * h, (p + s) * block:(p + s + 1) * block]
        result(j).start()

    own_mask.wait()

    @pl.loop(1, pairs + 1)
    def _(j):
        own(j).wait()

    for j, side in ((1, 1), (pairs, 0)):
        for s in steps:
            across(s, j).wait_recv()
            relay(side, s).start()
        convert(j)
    for side in (0, 1):
        mask_edge(side).wait_recv()
        edge(side).wait_recv()
        for s in steps:
            relay(side, s).wait_recv()
        convert(ends[side][1])

    @pl.loop(2, pairs)
    def _(j):
        for s in steps:
            across(s, j).wait_recv()
        convert(j)
        compute(j - 1)

    @pl.loop(pairs - 1, pairs + 1)
    def _(j):
        compute(j)

    for side in (0, 1):
        mask_edge(side).wait_send()
        edge(side).wait_send()
        for s in steps:
            relay(side, s).wait_send()

    @pl.loop(1, pairs + 1)
    def _(j):
        for s in steps:
            across(s, j).wait_send()
        result(j).wait()


def shards(cols, ring, density, pattern):
    rows, wide, h, block = density.shape
    pairs = rows // 2
    flags = pattern.astype(jnp.float32).reshape(pairs, 2, wide)
    flags = jnp.stack(
        [jnp.pad(flags[:, 0], ((0, 0), (0, 1))), jnp.pad(flags[:, 1], ((0, 0), (1, 0)))], axis=1)
    flags = jnp.pad(flags, ((0, 0), (0, 6), (0, 0)))
    mask = jnp.broadcast_to(flags[..., None], flags.shape + (block,)).reshape(pairs, 8, SLOTS * block)
    paired = density.reshape(pairs, 2, wide, h, block)
    width = SLOTS * block
    dma = pltpu.SemaphoreType.DMA
    out = pl.pallas_call(
        functools.partial(kernel, cols, ring),
        out_shape=jax.ShapeDtypeStruct(paired.shape, jnp.float32),
        in_specs=[pl.BlockSpec(memory_space=pl.ANY)] * 2,
        out_specs=pl.BlockSpec(memory_space=pl.ANY),
        scratch_shapes=[
            pltpu.VMEM((cols, pairs + 2, 2, wide, h, block), jnp.float32),
            pltpu.VMEM((pairs + 2, 8, width), jnp.float32),
            pltpu.VMEM((pairs + 2, 2 * block, width), jnp.bfloat16),
            pltpu.VMEM((pairs + 2, 2 * block, width), jnp.bfloat16),
            pltpu.VMEM(paired.shape, jnp.float32),
            dma((pairs,)),
            dma,
            dma((cols - 1, pairs)),
            dma((cols - 1, pairs)),
            dma((2,)),
            dma((2,)),
            dma((2, cols - 1)),
            dma((2, cols - 1)),
            dma((2,)),
            dma((2,)),
            dma((pairs,)),
        ],
        compiler_params=pltpu.CompilerParams(collective_id=0, has_side_effects=True),
    )(paired, mask)
    return out.reshape(density.shape)


def solution(mesh):
    cols = mesh.shape["col"]
    ring = mesh.shape["row"] * mesh.shape["depth"]
    in_specs = (P(RING, None, "col", None), P(RING, None))
    out_specs = P(RING, None, "col", None)
    body = functools.partial(shards, cols, ring)
    return jax.shard_map(body, mesh=mesh, in_specs=in_specs, out_specs=out_specs, check_vma=False)
```

```python
import functools

import jax
import jax.numpy as jnp
from jax import lax
from jax.experimental import pallas as pl
from jax.experimental.pallas import tpu as pltpu
from jax.sharding import PartitionSpec as P

MESH = pl.DeviceIdType.MESH
WIDE = 5
SLOTS = 6
RING = ("row", "depth")


def split(value):
    high = value.astype(jnp.bfloat16)
    low = (value - high.astype(jnp.float32)).astype(jnp.bfloat16)
    return high, low


def dot(a, b):
    return jnp.dot(a, b, preferred_element_type=jnp.float32)


def kernel(cols, ring, dens, pattern, out, raw, flags, masks, high, low,
           local_sem, flag_sem, send_sem, recv_sem, edge_send, edge_recv,
           relay_send, relay_recv, flag_send, flag_recv):
    pairs = dens.shape[0]
    h = dens.shape[3]
    block = dens.shape[4]
    two = 2 * block
    last = pairs + 1
    me = lax.axis_index("col")
    depth = lax.axis_size("depth")
    place = lax.axis_index("row") * depth + lax.axis_index("depth")

    def on_ring(shift):
        at = lax.rem(place + shift + ring, ring)
        return {"row": at // depth, "depth": lax.rem(at, depth)}

    prev, following = on_ring(-1), on_ring(1)

    def peer(step):
        return {"col": lax.rem(me + step, cols)}

    def source(step):
        return lax.rem(me + cols - step, cols)

    def own(j):
        return pltpu.make_async_copy(dens.at[j - 1], raw.at[me, j], local_sem.at[j - 1])

    def across(step, j):
        return pltpu.make_async_remote_copy(
            dens.at[j - 1], raw.at[me, j], send_sem.at[step - 1, j - 1],
            recv_sem.at[step - 1, j - 1], device_id=peer(step), device_id_type=MESH)

    ends = ((pairs, 0, following), (1, last, prev))

    def edge(side):
        j, slot, device = ends[side]
        return pltpu.make_async_remote_copy(
            dens.at[j - 1], raw.at[me, slot], edge_send.at[side], edge_recv.at[side],
            device_id=device, device_id_type=MESH)

    def relay(side, step):
        j, slot, device = ends[side]
        return pltpu.make_async_remote_copy(
            raw.at[source(step), j], raw.at[source(step), slot], relay_send.at[side, step - 1],
            relay_recv.at[side, step - 1], device_id=device, device_id_type=MESH)

    def flag_edge(side):
        return pltpu.make_async_remote_copy(
            pattern, flags.at[2 * side], flag_send.at[side], flag_recv.at[side],
            device_id=ends[side][2], device_id_type=MESH)

    steps = range(1, cols)

    barrier = pltpu.get_barrier_semaphore()
    for device in [peer(s) for s in steps] + [prev, following]:
        pl.semaphore_signal(barrier, inc=1, device_id=device, device_id_type=MESH)
    own_flags = pltpu.make_async_copy(pattern, flags.at[1], flag_sem)
    own_flags.start()
    pl.semaphore_wait(barrier, cols - 1 + 2)

    for j in (1, pairs):
        for s in steps:
            across(s, j).start()
    for side in (0, 1):
        flag_edge(side).start()
        edge(side).start()

    @pl.loop(2, pairs)
    def _(j):
        for s in steps:
            across(s, j).start()

    @pl.loop(1, pairs + 1)
    def _(j):
        own(j).start()

    def expand(which, i, j):
        lane = lax.broadcasted_iota(jnp.int32, flags.shape[1:], 1)
        for p in range(2):
            picked = jnp.where(lane == i + p, flags[which], 0).astype(jnp.float32)
            spread = jnp.broadcast_to(jnp.sum(picked, axis=1, keepdims=True), (WIDE, block))
            for s in range(WIDE):
                masks[j, p:p + 1, (p + s) * block:(p + s + 1) * block] = spread[s:s + 1]
            empty = slice(0, block) if p else slice(WIDE * block, SLOTS * block)
            masks[j, p:p + 1, empty] = jnp.zeros((1, block), jnp.float32)

    def convert(j):
        for p in range(2):
            for s in range(WIDE):
                slot = p + s
                factor = masks[j, p:p + 1, slot * block:(slot + 1) * block]
                for c in range(cols):
                    a, b = split(raw[c, j, p, s] * factor)
                    rows = slice(p * block + c * h, p * block + (c + 1) * h)
                    lanes = slice(slot * block, (slot + 1) * block)
                    high[j, rows, lanes] = a
                    low[j, rows, lanes] = b
            empty = slice(0, block) if p else slice(WIDE * block, SLOTS * block)
            nothing = jnp.zeros((block, block), jnp.bfloat16)
            high[j, p * block:(p + 1) * block, empty] = nothing
            low[j, p * block:(p + 1) * block, empty] = nothing

    def product(j, a, b):
        both = jnp.concatenate([a, b], axis=0)
        m = a.shape[0]
        parts = []
        for n in range(3):
            total = None
            for k in range(3):
                at = n - k + 1
                if at < 0 or at > 2:
                    continue
                lanes = slice(at * two, (at + 1) * two)
                ks = slice(k * two, (k + 1) * two)
                stacked = dot(both[:, ks], high[j + k - 1, :, lanes])
                term = stacked[:m] + stacked[m:] + dot(a[:, ks], low[j + k - 1, :, lanes])
                total = term if total is None else total + term
            parts.append(total)
        return jnp.concatenate(parts, axis=1)

    def compute(j):
        def own_rows(ref):
            return jnp.concatenate(
                [ref[j, pl.ds(pl.multiple_of(p * block + me * h, h), h), :] for p in range(2)], axis=0)

        factor = jnp.concatenate(
            [jnp.broadcast_to(masks[j, p:p + 1, :], (h, SLOTS * block)) for p in range(2)], axis=0)
        square = product(j, own_rows(high), own_rows(low)) * factor
        cube = product(j, *split(square)) * factor
        value = 3.0 * square - 2.0 * cube
        for p in range(2):
            for s in range(WIDE):
                out[j - 1, p, s] = value[p * h:(p + 1) * h, (p + s) * block:(p + s + 1) * block]

    own_flags.wait()

    @pl.loop(1, pairs + 1)
    def _(j):
        expand(1, 2 * (j - 1), j)

    for side in (0, 1):
        flag_edge(side).wait_recv()
    expand(0, 2 * (pairs - 1), 0)
    expand(2, 0, last)

    @pl.loop(1, pairs + 1)
    def _(j):
        own(j).wait()

    for j, side in ((1, 1), (pairs, 0)):
        for s in steps:
            across(s, j).wait_recv()
            relay(side, s).start()
        convert(j)
    for side in (0, 1):
        edge(side).wait_recv()
        for s in steps:
            relay(side, s).wait_recv()
        convert(ends[side][1])

    @pl.loop(2, pairs)
    def _(j):
        for s in steps:
            across(s, j).wait_recv()
        convert(j)
        compute(j - 1)

    @pl.loop(pairs - 1, pairs + 1)
    def _(j):
        compute(j)

    for side in (0, 1):
        flag_edge(side).wait_send()
        edge(side).wait_send()
        for s in steps:
            relay(side, s).wait_send()

    @pl.loop(1, pairs + 1)
    def _(j):
        for s in steps:
            across(s, j).wait_send()


def shards(cols, ring, density, pattern):
    rows, wide, h, block = density.shape
    pairs = rows // 2
    paired = density.reshape(pairs, 2, wide, h, block)
    width = SLOTS * block
    dma = pltpu.SemaphoreType.DMA
    out = pl.pallas_call(
        functools.partial(kernel, cols, ring),
        out_shape=pltpu.VMEM(paired.shape, jnp.float32),
        in_specs=[pl.BlockSpec(memory_space=pl.ANY)] * 2,
        out_specs=pl.BlockSpec(memory_space=pltpu.VMEM),
        scratch_shapes=[
            pltpu.VMEM((cols, pairs + 2, 2, wide, h, block), jnp.float32),
            pltpu.VMEM((3, wide, rows), jnp.int32),
            pltpu.VMEM((pairs + 2, 8, width), jnp.float32),
            pltpu.VMEM((pairs + 2, 2 * block, width), jnp.bfloat16),
            pltpu.VMEM((pairs + 2, 2 * block, width), jnp.bfloat16),
            dma((pairs,)),
            dma,
            dma((cols - 1, pairs)),
            dma((cols - 1, pairs)),
            dma((2,)),
            dma((2,)),
            dma((2, cols - 1)),
            dma((2, cols - 1)),
            dma((2,)),
            dma((2,)),
        ],
        compiler_params=pltpu.CompilerParams(
            collective_id=0, has_side_effects=True, vmem_limit_bytes=48 << 20),
    )(paired, pattern.T)
    return out.reshape(density.shape)


def solution(mesh):
    cols = mesh.shape["col"]
    ring = mesh.shape["row"] * mesh.shape["depth"]
    in_specs = (P(RING, None, "col", None), P(RING, None))
    out_specs = P(RING, None, "col", None)
    body = functools.partial(shards, cols, ring)
    return jax.shard_map(body, mesh=mesh, in_specs=in_specs, out_specs=out_specs, check_vma=False)
```

```python
import functools

import jax
import jax.numpy as jnp
from jax import lax
from jax.experimental import pallas as pl
from jax.experimental.pallas import tpu as pltpu
from jax.sharding import PartitionSpec as P

MESH = pl.DeviceIdType.MESH
WIDE = 5
SLOTS = 6
RING = ("row", "depth")


def split(value):
    high = value.astype(jnp.bfloat16)
    low = (value - high.astype(jnp.float32)).astype(jnp.bfloat16)
    return high, low


def dot(a, b):
    return jnp.dot(a, b, preferred_element_type=jnp.float32)


def products(block, h, me, masks, high, low, out):
    two = 2 * block

    def product(j, a, b):
        both = jnp.concatenate([a, b], axis=0)
        m = a.shape[0]
        parts = []
        for n in range(3):
            total = None
            for k in range(3):
                at = n - k + 1
                if at < 0 or at > 2:
                    continue
                lanes = slice(at * two, (at + 1) * two)
                ks = slice(k * two, (k + 1) * two)
                stacked = dot(both[:, ks], high[j + k - 1, :, lanes])
                term = stacked[:m] + stacked[m:] + dot(a[:, ks], low[j + k - 1, :, lanes])
                total = term if total is None else total + term
            parts.append(total)
        return jnp.concatenate(parts, axis=1)

    def compute(j, to):
        def own_rows(ref):
            return jnp.concatenate(
                [ref[j, pl.ds(pl.multiple_of(p * block + me * h, h), h), :] for p in range(2)], axis=0)

        factor = jnp.concatenate(
            [jnp.broadcast_to(masks[j, p:p + 1, :], (h, SLOTS * block)) for p in range(2)], axis=0)
        square = product(j, own_rows(high), own_rows(low)) * factor
        cube = product(j, *split(square)) * factor
        value = 3.0 * square - 2.0 * cube
        for p in range(2):
            for s in range(WIDE):
                out[to, p, s] = value[p * h:(p + 1) * h, (p + s) * block:(p + s + 1) * block]

    return compute


LATE = 3


def finish(masks, high, low, early, out, late, early_sem, late_sem):
    count, h, block = early.shape[0], early.shape[3], early.shape[4]
    me = lax.axis_index("col")
    first = pltpu.make_async_copy(early, out.at[pl.ds(0, count)], early_sem)
    first.start()
    compute = products(block, h, me, masks, high, low, late)

    def result(i):
        return pltpu.make_async_copy(late.at[i], out.at[count + i], late_sem.at[i])

    @pl.loop(0, LATE)
    def _(i):
        compute(count + 1 + i, i)
        result(i).start()

    first.wait()

    @pl.loop(0, LATE)
    def _(i):
        result(i).wait()


def kernel(cols, ring, dens, pattern, masks, high, low, early, raw, flags,
           local_sem, flag_sem, send_sem, recv_sem, edge_send, edge_recv,
           relay_send, relay_recv, flag_send, flag_recv):
    pairs = dens.shape[0]
    h = dens.shape[3]
    block = dens.shape[4]
    last = pairs + 1
    me = lax.axis_index("col")
    depth = lax.axis_size("depth")
    place = lax.axis_index("row") * depth + lax.axis_index("depth")

    def on_ring(shift):
        at = lax.rem(place + shift + ring, ring)
        return {"row": at // depth, "depth": lax.rem(at, depth)}

    prev, following = on_ring(-1), on_ring(1)

    def peer(step):
        return {"col": lax.rem(me + step, cols)}

    def source(step):
        return lax.rem(me + cols - step, cols)

    def own(j):
        return pltpu.make_async_copy(dens.at[j - 1], raw.at[me, j], local_sem.at[j - 1])

    def across(step, j):
        return pltpu.make_async_remote_copy(
            dens.at[j - 1], raw.at[me, j], send_sem.at[step - 1, j - 1],
            recv_sem.at[step - 1, j - 1], device_id=peer(step), device_id_type=MESH)

    ends = ((pairs, 0, following), (1, last, prev))

    def edge(side):
        j, slot, device = ends[side]
        return pltpu.make_async_remote_copy(
            dens.at[j - 1], raw.at[me, slot], edge_send.at[side], edge_recv.at[side],
            device_id=device, device_id_type=MESH)

    def relay(side, step):
        j, slot, device = ends[side]
        return pltpu.make_async_remote_copy(
            raw.at[source(step), j], raw.at[source(step), slot], relay_send.at[side, step - 1],
            relay_recv.at[side, step - 1], device_id=device, device_id_type=MESH)

    def flag_edge(side):
        return pltpu.make_async_remote_copy(
            pattern, flags.at[2 * side], flag_send.at[side], flag_recv.at[side],
            device_id=ends[side][2], device_id_type=MESH)

    steps = range(1, cols)

    barrier = pltpu.get_barrier_semaphore()
    for device in [peer(s) for s in steps] + [prev, following]:
        pl.semaphore_signal(barrier, inc=1, device_id=device, device_id_type=MESH)
    own_flags = pltpu.make_async_copy(pattern, flags.at[1], flag_sem)
    own_flags.start()
    pl.semaphore_wait(barrier, cols - 1 + 2)

    for j in (1, pairs):
        for s in steps:
            across(s, j).start()
    for side in (0, 1):
        flag_edge(side).start()
        edge(side).start()

    @pl.loop(2, pairs)
    def _(j):
        for s in steps:
            across(s, j).start()

    @pl.loop(1, pairs + 1)
    def _(j):
        own(j).start()

    def expand(which, i, j):
        lane = lax.broadcasted_iota(jnp.int32, flags.shape[1:], 1)
        for p in range(2):
            picked = jnp.where(lane == i + p, flags[which], 0).astype(jnp.float32)
            spread = jnp.broadcast_to(jnp.sum(picked, axis=1, keepdims=True), (WIDE, block))
            for s in range(WIDE):
                masks[j, p:p + 1, (p + s) * block:(p + s + 1) * block] = spread[s:s + 1]
            empty = slice(0, block) if p else slice(WIDE * block, SLOTS * block)
            masks[j, p:p + 1, empty] = jnp.zeros((1, block), jnp.float32)

    def convert(j):
        for p in range(2):
            for s in range(WIDE):
                slot = p + s
                factor = masks[j, p:p + 1, slot * block:(slot + 1) * block]
                for c in range(cols):
                    a, b = split(raw[c, j, p, s] * factor)
                    rows = slice(p * block + c * h, p * block + (c + 1) * h)
                    lanes = slice(slot * block, (slot + 1) * block)
                    high[j, rows, lanes] = a
                    low[j, rows, lanes] = b
            empty = slice(0, block) if p else slice(WIDE * block, SLOTS * block)
            nothing = jnp.zeros((block, block), jnp.bfloat16)
            high[j, p * block:(p + 1) * block, empty] = nothing
            low[j, p * block:(p + 1) * block, empty] = nothing

    compute = products(block, h, me, masks, high, low, early)

    own_flags.wait()

    @pl.loop(1, pairs + 1)
    def _(j):
        expand(1, 2 * (j - 1), j)

    for side in (0, 1):
        flag_edge(side).wait_recv()
    expand(0, 2 * (pairs - 1), 0)
    expand(2, 0, last)

    @pl.loop(1, pairs + 1)
    def _(j):
        own(j).wait()

    for j, side in ((1, 1), (pairs, 0)):
        for s in steps:
            across(s, j).wait_recv()
            relay(side, s).start()
        convert(j)
    for side in (0, 1):
        edge(side).wait_recv()
        for s in steps:
            relay(side, s).wait_recv()
        convert(ends[side][1])

    @pl.loop(2, pairs - 1)
    def _(j):
        for s in steps:
            across(s, j).wait_recv()
        convert(j)
        compute(j - 1, j - 2)

    for side in (0, 1):
        flag_edge(side).wait_send()
        edge(side).wait_send()
        for s in steps:
            relay(side, s).wait_send()
    for s in steps:
        across(s, pairs - 1).wait_recv()
    convert(pairs - 1)

    @pl.loop(1, pairs + 1)
    def _(j):
        for s in steps:
            across(s, j).wait_send()


def shards(cols, ring, density, pattern):
    rows, wide, h, block = density.shape
    pairs = rows // 2
    paired = density.reshape(pairs, 2, wide, h, block)
    width = SLOTS * block
    dma = pltpu.SemaphoreType.DMA
    vmem = pl.BlockSpec(memory_space=pltpu.VMEM)
    held = pl.pallas_call(
        functools.partial(kernel, cols, ring),
        out_shape=[
            pltpu.VMEM((pairs + 2, 8, width), jnp.float32),
            pltpu.VMEM((pairs + 2, 2 * block, width), jnp.bfloat16),
            pltpu.VMEM((pairs + 2, 2 * block, width), jnp.bfloat16),
            pltpu.VMEM((pairs - LATE,) + paired.shape[1:], jnp.float32),
        ],
        in_specs=[pl.BlockSpec(memory_space=pltpu.HBM)] * 2,
        out_specs=[vmem] * 4,
        scratch_shapes=[
            pltpu.VMEM((cols, pairs + 2, 2, wide, h, block), jnp.float32),
            pltpu.VMEM((3, wide, rows), jnp.int32),
            dma((pairs,)),
            dma,
            dma((cols - 1, pairs)),
            dma((cols - 1, pairs)),
            dma((2,)),
            dma((2,)),
            dma((2, cols - 1)),
            dma((2, cols - 1)),
            dma((2,)),
            dma((2,)),
        ],
        compiler_params=pltpu.CompilerParams(
            collective_id=0, has_side_effects=True, vmem_limit_bytes=42 << 20),
    )(*(pltpu.with_memory_space_constraint(x, pltpu.HBM) for x in (paired, pattern.T)))
    out = pl.pallas_call(
        finish,
        out_shape=jax.ShapeDtypeStruct(paired.shape, jnp.float32),
        in_specs=[vmem] * 4,
        out_specs=pl.BlockSpec(memory_space=pltpu.HBM),
        scratch_shapes=[
            pltpu.VMEM((LATE,) + paired.shape[1:], jnp.float32),
            dma,
            dma((LATE,)),
        ],
        compiler_params=pltpu.CompilerParams(vmem_limit_bytes=16 << 20),
    )(*held)
    return out.reshape(density.shape)


def solution(mesh):
    cols = mesh.shape["col"]
    ring = mesh.shape["row"] * mesh.shape["depth"]
    in_specs = (P(RING, None, "col", None), P(RING, None))
    out_specs = P(RING, None, "col", None)
    body = functools.partial(shards, cols, ring)
    return jax.shard_map(body, mesh=mesh, in_specs=in_specs, out_specs=out_specs, check_vma=False)
```

```python
import functools

import jax
import jax.numpy as jnp
from jax import lax
from jax.experimental import pallas as pl
from jax.experimental.pallas import tpu as pltpu
from jax.sharding import PartitionSpec as P

MESH = pl.DeviceIdType.MESH
WIDE = 5
SLOTS = 6
RING = ("row", "depth")


def split(value):
    high = value.astype(jnp.bfloat16)
    low = (value - high.astype(jnp.float32)).astype(jnp.bfloat16)
    return high, low


def dot(a, b):
    return jnp.dot(a, b, preferred_element_type=jnp.float32)


def products(block, h, me, masks, high, low, out):
    two = 2 * block

    def product(j, a, b):
        both = jnp.concatenate([a, b], axis=0)
        m = a.shape[0]
        parts = []
        for n in range(3):
            total = None
            for k in range(3):
                at = n - k + 1
                if at < 0 or at > 2:
                    continue
                lanes = slice(at * two, (at + 1) * two)
                ks = slice(k * two, (k + 1) * two)
                stacked = dot(both[:, ks], high[j + k - 1, :, lanes])
                term = stacked[:m] + stacked[m:] + dot(a[:, ks], low[j + k - 1, :, lanes])
                total = term if total is None else total + term
            parts.append(total)
        return jnp.concatenate(parts, axis=1)

    def compute(j, to):
        def own_rows(ref):
            return jnp.concatenate(
                [ref[j, pl.ds(pl.multiple_of(p * block + me * h, h), h), :] for p in range(2)], axis=0)

        factor = jnp.concatenate(
            [jnp.broadcast_to(masks[j, p:p + 1, :], (h, SLOTS * block)) for p in range(2)], axis=0)
        square = product(j, own_rows(high), own_rows(low)) * factor
        cube = product(j, *split(square)) * factor
        value = 3.0 * square - 2.0 * cube
        for p in range(2):
            for s in range(WIDE):
                out[to, p, s] = value[p * h:(p + 1) * h, (p + s) * block:(p + s + 1) * block]

    return compute


LATE = 3


def finish(masks, high, low, early, out, late, early_sem, late_sem):
    count, h, block = early.shape[0], early.shape[3], early.shape[4]
    me = lax.axis_index("col")
    first = pltpu.make_async_copy(early, out.at[pl.ds(0, count)], early_sem)
    first.start()
    compute = products(block, h, me, masks, high, low, late)

    def result(i):
        return pltpu.make_async_copy(late.at[i], out.at[count + i], late_sem.at[i])

    @pl.loop(0, LATE)
    def _(i):
        compute(count + 1 + i, i)
        result(i).start()

    first.wait()

    @pl.loop(0, LATE)
    def _(i):
        result(i).wait()


def kernel(cols, ring, dens, pattern, masks, high, low, early, raw, flags,
           local_sem, flag_sem, send_sem, recv_sem, edge_send, edge_recv,
           relay_send, relay_recv, flag_send, flag_recv, up, down, corner):
    pairs = dens.shape[0]
    h = dens.shape[3]
    block = dens.shape[4]
    last = pairs + 1
    me = lax.axis_index("col")
    depth = lax.axis_size("depth")
    place = lax.axis_index("row") * depth + lax.axis_index("depth")

    def on_ring(shift):
        at = lax.rem(place + shift + ring, ring)
        return {"row": at // depth, "depth": lax.rem(at, depth)}

    prev, following = on_ring(-1), on_ring(1)

    def peer(step):
        return {"col": lax.rem(me + step, cols)}

    def source(step):
        return lax.rem(me + cols - step, cols)

    def own(j):
        return pltpu.make_async_copy(dens.at[j - 1], raw.at[me, j], local_sem.at[j - 1])

    def across(step, j):
        return pltpu.make_async_remote_copy(
            dens.at[j - 1], raw.at[me, j], send_sem.at[step - 1, j - 1],
            recv_sem.at[step - 1, j - 1], device_id=peer(step), device_id_type=MESH)

    ends = ((pairs, 0, following), (1, last, prev))

    def edge(side):
        j, slot, device = ends[side]
        return pltpu.make_async_remote_copy(
            dens.at[j - 1], raw.at[me, slot], edge_send.at[side], edge_recv.at[side],
            device_id=device, device_id_type=MESH)

    def relay(side, step):
        j, slot, device = ends[side]
        return pltpu.make_async_remote_copy(
            raw.at[source(step), j], raw.at[source(step), slot], relay_send.at[side, step - 1],
            relay_recv.at[side, step - 1], device_id=device, device_id_type=MESH)

    def flag_edge(side):
        return pltpu.make_async_remote_copy(
            pattern, flags.at[2 * side], flag_send.at[side], flag_recv.at[side],
            device_id=ends[side][2], device_id_type=MESH)

    steps = range(1, cols)

    z, r = lax.axis_index("depth"), lax.axis_index("row")
    row_count = lax.axis_size("row")

    def greet(semaphore, device):
        pl.semaphore_signal(semaphore, inc=1, device_id=device, device_id_type=MESH)

    def along(step):
        return {"depth": z + step}

    def beside(step):
        return {"row": lax.rem(r + step + row_count, row_count)}

    barrier = pltpu.get_barrier_semaphore()
    for s in steps:
        greet(barrier, peer(s))

    @pl.when(z > 0)
    def _():
        greet(barrier, along(-1))

    @pl.when(z < depth - 1)
    def _():
        greet(barrier, along(1))

    @pl.when(z == 0)
    def _():
        greet(barrier, beside(-1))
        greet(barrier, beside(1))

    own_flags = pltpu.make_async_copy(pattern, flags.at[1], flag_sem)
    own_flags.start()
    near = jnp.where(z == 0, 2, 1) + jnp.where(z < depth - 1, 1, 0)
    pl.semaphore_wait(barrier, cols - 1 + near)

    for j in (1, pairs):
        for s in steps:
            across(s, j).start()

    @pl.loop(2, pairs)
    def _(j):
        for s in steps:
            across(s, j).start()

    @pl.when(z > 0)
    def _():
        pl.semaphore_wait(up, 1)

    @pl.when(z < depth - 1)
    def _():
        greet(up, along(1))

    @pl.when(z < depth - 2)
    def _():
        pl.semaphore_wait(down, 1)

    @pl.when((z > 0) & (z <= depth - 2))
    def _():
        greet(down, along(-1))

    @pl.when(z == 0)
    def _():
        greet(corner, beside(1))
        pl.semaphore_wait(corner, 1)

    for side in (0, 1):
        flag_edge(side).start()
        edge(side).start()

    @pl.loop(1, pairs + 1)
    def _(j):
        own(j).start()

    def expand(which, i, j):
        lane = lax.broadcasted_iota(jnp.int32, flags.shape[1:], 1)
        for p in range(2):
            picked = jnp.where(lane == i + p, flags[which], 0).astype(jnp.float32)
            spread = jnp.broadcast_to(jnp.sum(picked, axis=1, keepdims=True), (WIDE, block))
            for s in range(WIDE):
                masks[j, p:p + 1, (p + s) * block:(p + s + 1) * block] = spread[s:s + 1]
            empty = slice(0, block) if p else slice(WIDE * block, SLOTS * block)
            masks[j, p:p + 1, empty] = jnp.zeros((1, block), jnp.float32)

    def convert(j):
        for p in range(2):
            for s in range(WIDE):
                slot = p + s
                factor = masks[j, p:p + 1, slot * block:(slot + 1) * block]
                for c in range(cols):
                    a, b = split(raw[c, j, p, s] * factor)
                    rows = slice(p * block + c * h, p * block + (c + 1) * h)
                    lanes = slice(slot * block, (slot + 1) * block)
                    high[j, rows, lanes] = a
                    low[j, rows, lanes] = b
            empty = slice(0, block) if p else slice(WIDE * block, SLOTS * block)
            nothing = jnp.zeros((block, block), jnp.bfloat16)
            high[j, p * block:(p + 1) * block, empty] = nothing
            low[j, p * block:(p + 1) * block, empty] = nothing

    compute = products(block, h, me, masks, high, low, early)

    own_flags.wait()

    @pl.loop(1, pairs + 1)
    def _(j):
        expand(1, 2 * (j - 1), j)

    for side in (0, 1):
        flag_edge(side).wait_recv()
    expand(0, 2 * (pairs - 1), 0)
    expand(2, 0, last)

    @pl.loop(1, pairs + 1)
    def _(j):
        own(j).wait()

    for j, side in ((1, 1), (pairs, 0)):
        for s in steps:
            across(s, j).wait_recv()
            relay(side, s).start()
        convert(j)
    for side in (0, 1):
        edge(side).wait_recv()
        for s in steps:
            relay(side, s).wait_recv()
        convert(ends[side][1])

    @pl.loop(2, pairs - 1)
    def _(j):
        for s in steps:
            across(s, j).wait_recv()
        convert(j)
        compute(j - 1, j - 2)

    for side in (0, 1):
        flag_edge(side).wait_send()
        edge(side).wait_send()
        for s in steps:
            relay(side, s).wait_send()
    for s in steps:
        across(s, pairs - 1).wait_recv()
    convert(pairs - 1)

    @pl.loop(1, pairs + 1)
    def _(j):
        for s in steps:
            across(s, j).wait_send()


def shards(cols, ring, density, pattern):
    rows, wide, h, block = density.shape
    pairs = rows // 2
    paired = density.reshape(pairs, 2, wide, h, block)
    width = SLOTS * block
    dma = pltpu.SemaphoreType.DMA
    vmem = pl.BlockSpec(memory_space=pltpu.VMEM)
    held = pl.pallas_call(
        functools.partial(kernel, cols, ring),
        out_shape=[
            pltpu.VMEM((pairs + 2, 8, width), jnp.float32),
            pltpu.VMEM((pairs + 2, 2 * block, width), jnp.bfloat16),
            pltpu.VMEM((pairs + 2, 2 * block, width), jnp.bfloat16),
            pltpu.VMEM((pairs - LATE,) + paired.shape[1:], jnp.float32),
        ],
        in_specs=[pl.BlockSpec(memory_space=pltpu.HBM)] * 2,
        out_specs=[vmem] * 4,
        scratch_shapes=[
            pltpu.VMEM((cols, pairs + 2, 2, wide, h, block), jnp.float32),
            pltpu.VMEM((3, wide, rows), jnp.int32),
            dma((pairs,)),
            dma,
            dma((cols - 1, pairs)),
            dma((cols - 1, pairs)),
            dma((2,)),
            dma((2,)),
            dma((2, cols - 1)),
            dma((2, cols - 1)),
            dma((2,)),
            dma((2,)),
            pltpu.SemaphoreType.REGULAR,
            pltpu.SemaphoreType.REGULAR,
            pltpu.SemaphoreType.REGULAR,
        ],
        compiler_params=pltpu.CompilerParams(
            collective_id=0, has_side_effects=True, vmem_limit_bytes=42 << 20),
    )(*(pltpu.with_memory_space_constraint(x, pltpu.HBM) for x in (paired, pattern.T)))
    out = pl.pallas_call(
        finish,
        out_shape=jax.ShapeDtypeStruct(paired.shape, jnp.float32),
        in_specs=[vmem] * 4,
        out_specs=pl.BlockSpec(memory_space=pltpu.HBM),
        scratch_shapes=[
            pltpu.VMEM((LATE,) + paired.shape[1:], jnp.float32),
            dma,
            dma((LATE,)),
        ],
        compiler_params=pltpu.CompilerParams(vmem_limit_bytes=16 << 20),
    )(*held)
    return out.reshape(density.shape)


def solution(mesh):
    cols = mesh.shape["col"]
    ring = mesh.shape["row"] * mesh.shape["depth"]
    in_specs = (P(RING, None, "col", None), P(RING, None))
    out_specs = P(RING, None, "col", None)
    body = functools.partial(shards, cols, ring)
    return jax.shard_map(body, mesh=mesh, in_specs=in_specs, out_specs=out_specs, check_vma=False)
```

```python
import functools

import jax
import jax.numpy as jnp
from jax import lax
from jax.experimental import pallas as pl
from jax.experimental.pallas import tpu as pltpu
from jax.sharding import PartitionSpec as P

MESH = pl.DeviceIdType.MESH
WIDE = 5
SLOTS = 6
RING = ("row", "depth")


def split(value):
    high = value.astype(jnp.bfloat16)
    low = (value - high.astype(jnp.float32)).astype(jnp.bfloat16)
    return high, low


def dot(a, b):
    return jnp.dot(a, b, preferred_element_type=jnp.float32)


def products(block, h, me, masks, high, low, out):
    two = 2 * block

    def product(j, a, b, sources=(0, 1, 2), start=None):
        both = jnp.concatenate([a, b], axis=0)
        m = a.shape[0]
        parts = []
        for n in range(3):
            total = None if start is None else start[:, n * two:(n + 1) * two]
            for k in sources:
                at = n - k + 1
                if at < 0 or at > 2:
                    continue
                lanes = slice(at * two, (at + 1) * two)
                ks = slice(k * two, (k + 1) * two)
                stacked = dot(both[:, ks], high[j + k - 1, :, lanes])
                term = stacked[:m] + stacked[m:] + dot(a[:, ks], low[j + k - 1, :, lanes])
                total = term if total is None else total + term
            parts.append(total)
        return jnp.concatenate(parts, axis=1)

    def own_rows(ref, j):
        return jnp.concatenate(
            [ref[j, pl.ds(pl.multiple_of(p * block + me * h, h), h), :] for p in range(2)], axis=0)

    def compute(j, to, sources=(0, 1, 2), start=None):
        factor = jnp.concatenate(
            [jnp.broadcast_to(masks[j, p:p + 1, :], (h, SLOTS * block)) for p in range(2)], axis=0)
        square = product(j, own_rows(high, j), own_rows(low, j), sources, start) * factor
        cube = product(j, *split(square)) * factor
        value = 3.0 * square - 2.0 * cube
        for p in range(2):
            for s in range(WIDE):
                out[to, p, s] = value[p * h:(p + 1) * h, (p + s) * block:(p + s + 1) * block]

    return product, own_rows, compute


BEFORE = ((0, 1), (0, 2), (1, 2))
AFTER = ((2,), (1,), (0,))
LATE = 3


def finish(masks, high, low, early, begun, out, late, early_sem, late_sem):
    count, h, block = early.shape[0], early.shape[3], early.shape[4]
    me = lax.axis_index("col")
    first = pltpu.make_async_copy(early, out.at[pl.ds(0, count)], early_sem)
    first.start()
    _, _, compute = products(block, h, me, masks, high, low, late)

    def result(i):
        return pltpu.make_async_copy(late.at[i], out.at[count + i], late_sem.at[i])

    for i in range(LATE):
        compute(count + 1 + i, i, AFTER[i], begun[i])
        result(i).start()

    first.wait()

    @pl.loop(0, LATE)
    def _(i):
        result(i).wait()


def kernel(cols, ring, dens, pattern, masks, high, low, early, begun, raw, flags,
           local_sem, flag_sem, send_sem, recv_sem, edge_send, edge_recv,
           relay_send, relay_recv, flag_send, flag_recv, up, down, corner):
    pairs = dens.shape[0]
    h = dens.shape[3]
    block = dens.shape[4]
    last = pairs + 1
    me = lax.axis_index("col")
    depth = lax.axis_size("depth")
    place = lax.axis_index("row") * depth + lax.axis_index("depth")

    def on_ring(shift):
        at = lax.rem(place + shift + ring, ring)
        return {"row": at // depth, "depth": lax.rem(at, depth)}

    prev, following = on_ring(-1), on_ring(1)

    def peer(step):
        return {"col": lax.rem(me + step, cols)}

    def source(step):
        return lax.rem(me + cols - step, cols)

    def own(j):
        return pltpu.make_async_copy(dens.at[j - 1], raw.at[me, j], local_sem.at[j - 1])

    def across(step, j):
        return pltpu.make_async_remote_copy(
            dens.at[j - 1], raw.at[me, j], send_sem.at[step - 1, j - 1],
            recv_sem.at[step - 1, j - 1], device_id=peer(step), device_id_type=MESH)

    ends = ((pairs, 0, following), (1, last, prev))

    def edge(side):
        j, slot, device = ends[side]
        return pltpu.make_async_remote_copy(
            dens.at[j - 1], raw.at[me, slot], edge_send.at[side], edge_recv.at[side],
            device_id=device, device_id_type=MESH)

    def relay(side, step):
        j, slot, device = ends[side]
        return pltpu.make_async_remote_copy(
            raw.at[source(step), j], raw.at[source(step), slot], relay_send.at[side, step - 1],
            relay_recv.at[side, step - 1], device_id=device, device_id_type=MESH)

    def flag_edge(side):
        return pltpu.make_async_remote_copy(
            pattern, flags.at[2 * side], flag_send.at[side], flag_recv.at[side],
            device_id=ends[side][2], device_id_type=MESH)

    steps = range(1, cols)

    z, r = lax.axis_index("depth"), lax.axis_index("row")
    row_count = lax.axis_size("row")

    def greet(semaphore, device):
        pl.semaphore_signal(semaphore, inc=1, device_id=device, device_id_type=MESH)

    def along(step):
        return {"depth": z + step}

    def beside(step):
        return {"row": lax.rem(r + step + row_count, row_count)}

    barrier = pltpu.get_barrier_semaphore()
    for s in steps:
        greet(barrier, peer(s))

    @pl.when(z > 0)
    def _():
        greet(barrier, along(-1))

    @pl.when(z < depth - 1)
    def _():
        greet(barrier, along(1))

    @pl.when(z == 0)
    def _():
        greet(barrier, beside(-1))
        greet(barrier, beside(1))

    own_flags = pltpu.make_async_copy(pattern, flags.at[1], flag_sem)
    own_flags.start()
    near = jnp.where(z == 0, 2, 1) + jnp.where(z < depth - 1, 1, 0)
    pl.semaphore_wait(barrier, cols - 1 + near)

    for j in (1, pairs):
        for s in steps:
            across(s, j).start()

    @pl.loop(2, pairs)
    def _(j):
        for s in steps:
            across(s, j).start()

    @pl.when(z > 0)
    def _():
        pl.semaphore_wait(up, 1)

    @pl.when(z < depth - 1)
    def _():
        greet(up, along(1))

    @pl.when(z < depth - 2)
    def _():
        pl.semaphore_wait(down, 1)

    @pl.when((z > 0) & (z <= depth - 2))
    def _():
        greet(down, along(-1))

    @pl.when(z == 0)
    def _():
        greet(corner, beside(1))
        pl.semaphore_wait(corner, 1)

    for side in (0, 1):
        flag_edge(side).start()
        edge(side).start()

    @pl.loop(1, pairs + 1)
    def _(j):
        own(j).start()

    def expand(which, i, j):
        lane = lax.broadcasted_iota(jnp.int32, flags.shape[1:], 1)
        for p in range(2):
            picked = jnp.where(lane == i + p, flags[which], 0).astype(jnp.float32)
            spread = jnp.broadcast_to(jnp.sum(picked, axis=1, keepdims=True), (WIDE, block))
            for s in range(WIDE):
                masks[j, p:p + 1, (p + s) * block:(p + s + 1) * block] = spread[s:s + 1]
            empty = slice(0, block) if p else slice(WIDE * block, SLOTS * block)
            masks[j, p:p + 1, empty] = jnp.zeros((1, block), jnp.float32)

    def convert(j):
        for p in range(2):
            for s in range(WIDE):
                slot = p + s
                factor = masks[j, p:p + 1, slot * block:(slot + 1) * block]
                for c in range(cols):
                    a, b = split(raw[c, j, p, s] * factor)
                    rows = slice(p * block + c * h, p * block + (c + 1) * h)
                    lanes = slice(slot * block, (slot + 1) * block)
                    high[j, rows, lanes] = a
                    low[j, rows, lanes] = b
            empty = slice(0, block) if p else slice(WIDE * block, SLOTS * block)
            nothing = jnp.zeros((block, block), jnp.bfloat16)
            high[j, p * block:(p + 1) * block, empty] = nothing
            low[j, p * block:(p + 1) * block, empty] = nothing

    product, own_rows, compute = products(block, h, me, masks, high, low, early)

    own_flags.wait()

    @pl.loop(1, pairs + 1)
    def _(j):
        expand(1, 2 * (j - 1), j)

    for side in (0, 1):
        flag_edge(side).wait_recv()
    expand(0, 2 * (pairs - 1), 0)
    expand(2, 0, last)

    @pl.loop(1, pairs + 1)
    def _(j):
        own(j).wait()

    for j, side in ((1, 1), (pairs, 0)):
        for s in steps:
            across(s, j).wait_recv()
            relay(side, s).start()
        convert(j)
    for side in (0, 1):
        edge(side).wait_recv()
        for s in steps:
            relay(side, s).wait_recv()
        convert(ends[side][1])

    @pl.loop(2, pairs - 1)
    def _(j):
        for s in steps:
            across(s, j).wait_recv()
        convert(j)
        compute(j - 1, j - 2)

    def local_rows(j):
        rows = []
        for p in range(2):
            blocks = [raw[me, j, p, s] for s in range(WIDE)]
            empty = [jnp.zeros((h, block), jnp.float32)]
            row = jnp.concatenate(empty + blocks if p else blocks + empty, axis=1)
            rows.append(row * masks[j, p:p + 1, :])
        return split(jnp.concatenate(rows, axis=0))

    for i in range(LATE):
        j = pairs - LATE + 1 + i
        a, b = local_rows(j) if i == 1 else (own_rows(high, j), own_rows(low, j))
        begun[i] = product(j, a, b, BEFORE[i])

    for side in (0, 1):
        flag_edge(side).wait_send()
        edge(side).wait_send()
        for s in steps:
            relay(side, s).wait_send()
    for s in steps:
        across(s, pairs - 1).wait_recv()
    convert(pairs - 1)

    @pl.loop(1, pairs + 1)
    def _(j):
        for s in steps:
            across(s, j).wait_send()


def shards(cols, ring, density, pattern):
    rows, wide, h, block = density.shape
    pairs = rows // 2
    paired = density.reshape(pairs, 2, wide, h, block)
    width = SLOTS * block
    dma = pltpu.SemaphoreType.DMA
    vmem = pl.BlockSpec(memory_space=pltpu.VMEM)
    held = pl.pallas_call(
        functools.partial(kernel, cols, ring),
        out_shape=[
            pltpu.VMEM((pairs + 2, 8, width), jnp.float32),
            pltpu.VMEM((pairs + 2, 2 * block, width), jnp.bfloat16),
            pltpu.VMEM((pairs + 2, 2 * block, width), jnp.bfloat16),
            pltpu.VMEM((pairs - LATE,) + paired.shape[1:], jnp.float32),
            pltpu.VMEM((LATE, 2 * h, width), jnp.float32),
        ],
        in_specs=[pl.BlockSpec(memory_space=pltpu.HBM)] * 2,
        out_specs=[vmem] * 5,
        scratch_shapes=[
            pltpu.VMEM((cols, pairs + 2, 2, wide, h, block), jnp.float32),
            pltpu.VMEM((3, wide, rows), jnp.int32),
            dma((pairs,)),
            dma,
            dma((cols - 1, pairs)),
            dma((cols - 1, pairs)),
            dma((2,)),
            dma((2,)),
            dma((2, cols - 1)),
            dma((2, cols - 1)),
            dma((2,)),
            dma((2,)),
            pltpu.SemaphoreType.REGULAR,
            pltpu.SemaphoreType.REGULAR,
            pltpu.SemaphoreType.REGULAR,
        ],
        compiler_params=pltpu.CompilerParams(
            collective_id=0, has_side_effects=True, vmem_limit_bytes=42 << 20),
    )(*(pltpu.with_memory_space_constraint(x, pltpu.HBM) for x in (paired, pattern.T)))
    out = pl.pallas_call(
        finish,
        out_shape=jax.ShapeDtypeStruct(paired.shape, jnp.float32),
        in_specs=[vmem] * 5,
        out_specs=pl.BlockSpec(memory_space=pltpu.HBM),
        scratch_shapes=[
            pltpu.VMEM((LATE,) + paired.shape[1:], jnp.float32),
            dma,
            dma((LATE,)),
        ],
        compiler_params=pltpu.CompilerParams(vmem_limit_bytes=16 << 20),
    )(*held)
    return out.reshape(density.shape)


def solution(mesh):
    cols = mesh.shape["col"]
    ring = mesh.shape["row"] * mesh.shape["depth"]
    in_specs = (P(RING, None, "col", None), P(RING, None))
    out_specs = P(RING, None, "col", None)
    body = functools.partial(shards, cols, ring)
    return jax.shard_map(body, mesh=mesh, in_specs=in_specs, out_specs=out_specs, check_vma=False)
```

```python
import functools

import jax
import jax.numpy as jnp
from jax import lax
from jax.experimental import pallas as pl
from jax.experimental.pallas import tpu as pltpu
from jax.sharding import PartitionSpec as P

MESH = pl.DeviceIdType.MESH
WIDE = 5
SLOTS = 6
RING = ("row", "depth")


def split(value):
    high = value.astype(jnp.bfloat16)
    low = (value - high.astype(jnp.float32)).astype(jnp.bfloat16)
    return high, low


def dot(a, b):
    return jnp.dot(a, b, preferred_element_type=jnp.float32)


def products(block, h, me, masks, high, low, out):
    two = 2 * block

    def product(j, a, b, sources=(0, 1, 2), start=None):
        both = jnp.concatenate([a, b], axis=0)
        m = a.shape[0]
        parts = []
        for n in range(3):
            total = None if start is None else start[:, n * two:(n + 1) * two]
            for k in sources:
                at = n - k + 1
                if at < 0 or at > 2:
                    continue
                lanes = slice(at * two, (at + 1) * two)
                ks = slice(k * two, (k + 1) * two)
                stacked = dot(both[:, ks], high[j + k - 1, :, lanes])
                term = stacked[:m] + stacked[m:] + dot(a[:, ks], low[j + k - 1, :, lanes])
                total = term if total is None else total + term
            parts.append(total)
        return jnp.concatenate(parts, axis=1)

    def own_rows(ref, j):
        return jnp.concatenate(
            [ref[j, pl.ds(pl.multiple_of(p * block + me * h, h), h), :] for p in range(2)], axis=0)

    def compute(j, to, sources=(0, 1, 2), start=None):
        factor = jnp.concatenate(
            [jnp.broadcast_to(masks[j, p:p + 1, :], (h, SLOTS * block)) for p in range(2)], axis=0)
        square = product(j, own_rows(high, j), own_rows(low, j), sources, start) * factor
        cube = product(j, *split(square)) * factor
        value = 3.0 * square - 2.0 * cube
        for p in range(2):
            for s in range(WIDE):
                out[to, p, s] = value[p * h:(p + 1) * h, (p + s) * block:(p + s + 1) * block]

    return product, own_rows, compute


BEFORE = ((0, 1), (0, 2), (1, 2))
AFTER = ((2,), (1,), (0,))
LATE = 3


def finish(masks, high, low, early, begun, out, late, early_sem, late_sem):
    count, h, block = early.shape[0], early.shape[3], early.shape[4]
    me = lax.axis_index("col")
    def ready(i):
        return pltpu.make_async_copy(early.at[i], out.at[i], early_sem.at[i])

    for i in range(count):
        ready(i).start()
    _, _, compute = products(block, h, me, masks, high, low, late)

    def result(i):
        return pltpu.make_async_copy(late.at[i], out.at[count + i], late_sem.at[i])

    for i in range(LATE):
        compute(count + 1 + i, i, AFTER[i], begun[i])
        result(i).start()

    for i in range(count):
        ready(i).wait()

    @pl.loop(0, LATE)
    def _(i):
        result(i).wait()


def kernel(cols, ring, dens, pattern, masks, high, low, early, begun, raw, flags,
           local_sem, flag_sem, send_sem, recv_sem, edge_send, edge_recv,
           relay_send, relay_recv, flag_send, flag_recv, up, down, corner):
    pairs = dens.shape[0]
    h = dens.shape[3]
    block = dens.shape[4]
    last = pairs + 1
    me = lax.axis_index("col")
    depth = lax.axis_size("depth")
    place = lax.axis_index("row") * depth + lax.axis_index("depth")

    def on_ring(shift):
        at = lax.rem(place + shift + ring, ring)
        return {"row": at // depth, "depth": lax.rem(at, depth)}

    prev, following = on_ring(-1), on_ring(1)

    def peer(step):
        return {"col": lax.rem(me + step, cols)}

    def source(step):
        return lax.rem(me + cols - step, cols)

    def own(j):
        return pltpu.make_async_copy(dens.at[j - 1], raw.at[me, j], local_sem.at[j - 1])

    def across(step, j):
        return pltpu.make_async_remote_copy(
            dens.at[j - 1], raw.at[me, j], send_sem.at[step - 1, j - 1],
            recv_sem.at[step - 1, j - 1], device_id=peer(step), device_id_type=MESH)

    ends = ((pairs, 0, following), (1, last, prev))

    def edge(side):
        j, slot, device = ends[side]
        return pltpu.make_async_remote_copy(
            dens.at[j - 1], raw.at[me, slot], edge_send.at[side], edge_recv.at[side],
            device_id=device, device_id_type=MESH)

    def relay(side, step):
        j, slot, device = ends[side]
        return pltpu.make_async_remote_copy(
            raw.at[source(step), j], raw.at[source(step), slot], relay_send.at[side, step - 1],
            relay_recv.at[side, step - 1], device_id=device, device_id_type=MESH)

    def flag_edge(side):
        return pltpu.make_async_remote_copy(
            pattern, flags.at[2 * side], flag_send.at[side], flag_recv.at[side],
            device_id=ends[side][2], device_id_type=MESH)

    steps = range(1, cols)

    z, r = lax.axis_index("depth"), lax.axis_index("row")
    row_count = lax.axis_size("row")

    def greet(semaphore, device):
        pl.semaphore_signal(semaphore, inc=1, device_id=device, device_id_type=MESH)

    def along(step):
        return {"depth": z + step}

    def beside(step):
        return {"row": lax.rem(r + step + row_count, row_count)}

    barrier = pltpu.get_barrier_semaphore()
    for s in steps:
        greet(barrier, peer(s))

    @pl.when(z > 0)
    def _():
        greet(barrier, along(-1))

    @pl.when(z < depth - 1)
    def _():
        greet(barrier, along(1))

    @pl.when(z == 0)
    def _():
        greet(barrier, beside(-1))
        greet(barrier, beside(1))

    own_flags = pltpu.make_async_copy(pattern, flags.at[1], flag_sem)
    own_flags.start()
    near = jnp.where(z == 0, 2, 1) + jnp.where(z < depth - 1, 1, 0)
    pl.semaphore_wait(barrier, cols - 1 + near)

    for j in (1, pairs):
        for s in steps:
            across(s, j).start()

    @pl.loop(2, pairs)
    def _(j):
        for s in steps:
            across(s, j).start()

    @pl.when(z > 0)
    def _():
        pl.semaphore_wait(up, 1)

    @pl.when(z < depth - 1)
    def _():
        greet(up, along(1))

    @pl.when(z < depth - 2)
    def _():
        pl.semaphore_wait(down, 1)

    @pl.when((z > 0) & (z <= depth - 2))
    def _():
        greet(down, along(-1))

    @pl.when(z == 0)
    def _():
        greet(corner, beside(1))
        pl.semaphore_wait(corner, 1)

    for side in (0, 1):
        flag_edge(side).start()
        edge(side).start()

    @pl.loop(1, pairs + 1)
    def _(j):
        own(j).start()

    def expand(which, i, j):
        lane = lax.broadcasted_iota(jnp.int32, flags.shape[1:], 1)
        for p in range(2):
            picked = jnp.where(lane == i + p, flags[which], 0).astype(jnp.float32)
            spread = jnp.broadcast_to(jnp.sum(picked, axis=1, keepdims=True), (WIDE, block))
            for s in range(WIDE):
                masks[j, p:p + 1, (p + s) * block:(p + s + 1) * block] = spread[s:s + 1]
            empty = slice(0, block) if p else slice(WIDE * block, SLOTS * block)
            masks[j, p:p + 1, empty] = jnp.zeros((1, block), jnp.float32)

    def convert(j):
        for p in range(2):
            for s in range(WIDE):
                slot = p + s
                factor = masks[j, p:p + 1, slot * block:(slot + 1) * block]
                for c in range(cols):
                    a, b = split(raw[c, j, p, s] * factor)
                    rows = slice(p * block + c * h, p * block + (c + 1) * h)
                    lanes = slice(slot * block, (slot + 1) * block)
                    high[j, rows, lanes] = a
                    low[j, rows, lanes] = b
            empty = slice(0, block) if p else slice(WIDE * block, SLOTS * block)
            nothing = jnp.zeros((block, block), jnp.bfloat16)
            high[j, p * block:(p + 1) * block, empty] = nothing
            low[j, p * block:(p + 1) * block, empty] = nothing

    product, own_rows, compute = products(block, h, me, masks, high, low, early)

    own_flags.wait()

    @pl.loop(1, pairs + 1)
    def _(j):
        expand(1, 2 * (j - 1), j)

    for side in (0, 1):
        flag_edge(side).wait_recv()
    expand(0, 2 * (pairs - 1), 0)
    expand(2, 0, last)

    @pl.loop(1, pairs + 1)
    def _(j):
        own(j).wait()

    for j, side in ((1, 1), (pairs, 0)):
        for s in steps:
            across(s, j).wait_recv()
            relay(side, s).start()
        convert(j)
    for side in (0, 1):
        edge(side).wait_recv()
        for s in steps:
            relay(side, s).wait_recv()
        convert(ends[side][1])

    @pl.loop(2, pairs - 1)
    def _(j):
        for s in steps:
            across(s, j).wait_recv()
        convert(j)
        compute(j - 1, j - 2)

    def local_rows(j):
        rows = []
        for p in range(2):
            blocks = [raw[me, j, p, s] for s in range(WIDE)]
            empty = [jnp.zeros((h, block), jnp.float32)]
            row = jnp.concatenate(empty + blocks if p else blocks + empty, axis=1)
            rows.append(row * masks[j, p:p + 1, :])
        return split(jnp.concatenate(rows, axis=0))

    for i in range(LATE):
        j = pairs - LATE + 1 + i
        a, b = local_rows(j) if i == 1 else (own_rows(high, j), own_rows(low, j))
        begun[i] = product(j, a, b, BEFORE[i])

    for side in (0, 1):
        flag_edge(side).wait_send()
        edge(side).wait_send()
        for s in steps:
            relay(side, s).wait_send()
    for s in steps:
        across(s, pairs - 1).wait_recv()
    convert(pairs - 1)

    @pl.loop(1, pairs + 1)
    def _(j):
        for s in steps:
            across(s, j).wait_send()


def shards(cols, ring, density, pattern):
    rows, wide, h, block = density.shape
    pairs = rows // 2
    paired = density.reshape(pairs, 2, wide, h, block)
    width = SLOTS * block
    dma = pltpu.SemaphoreType.DMA
    vmem = pl.BlockSpec(memory_space=pltpu.VMEM)
    held = pl.pallas_call(
        functools.partial(kernel, cols, ring),
        out_shape=[
            pltpu.VMEM((pairs + 2, 8, width), jnp.float32),
            pltpu.VMEM((pairs + 2, 2 * block, width), jnp.bfloat16),
            pltpu.VMEM((pairs + 2, 2 * block, width), jnp.bfloat16),
            pltpu.VMEM((pairs - LATE,) + paired.shape[1:], jnp.float32),
            pltpu.VMEM((LATE, 2 * h, width), jnp.float32),
        ],
        in_specs=[pl.BlockSpec(memory_space=pltpu.HBM)] * 2,
        out_specs=[vmem] * 5,
        scratch_shapes=[
            pltpu.VMEM((cols, pairs + 2, 2, wide, h, block), jnp.float32),
            pltpu.VMEM((3, wide, rows), jnp.int32),
            dma((pairs,)),
            dma,
            dma((cols - 1, pairs)),
            dma((cols - 1, pairs)),
            dma((2,)),
            dma((2,)),
            dma((2, cols - 1)),
            dma((2, cols - 1)),
            dma((2,)),
            dma((2,)),
            pltpu.SemaphoreType.REGULAR,
            pltpu.SemaphoreType.REGULAR,
            pltpu.SemaphoreType.REGULAR,
        ],
        compiler_params=pltpu.CompilerParams(
            collective_id=0, has_side_effects=True, vmem_limit_bytes=42 << 20),
    )(*(pltpu.with_memory_space_constraint(x, pltpu.HBM) for x in (paired, pattern.T)))
    out = pl.pallas_call(
        finish,
        out_shape=jax.ShapeDtypeStruct(paired.shape, jnp.float32),
        in_specs=[vmem] * 5,
        out_specs=pl.BlockSpec(memory_space=pltpu.HBM),
        scratch_shapes=[
            pltpu.VMEM((LATE,) + paired.shape[1:], jnp.float32),
            dma((pairs - LATE,)),
            dma((LATE,)),
        ],
        compiler_params=pltpu.CompilerParams(vmem_limit_bytes=16 << 20),
    )(*held)
    return out.reshape(density.shape)


def solution(mesh):
    cols = mesh.shape["col"]
    ring = mesh.shape["row"] * mesh.shape["depth"]
    in_specs = (P(RING, None, "col", None), P(RING, None))
    out_specs = P(RING, None, "col", None)
    body = functools.partial(shards, cols, ring)
    return jax.shard_map(body, mesh=mesh, in_specs=in_specs, out_specs=out_specs, check_vma=False)
```
